32 devices in a mesh: front: 4 (over z), row: 4 (over x, core), col: 2 (over y).
Axes of the slice: x: 2, y: 2, z: 4, core: 2. Of those that a mesh axis runs over, the one named last changes fastest.
Arguments:
- front_slab: bfloat16 [4, 2048, 8192], P('front', 'row', 'col'), may hold values from -0.0625 to 0.0625
- samples: bfloat16 [8192, 256], P(('row', 'col')), may hold values from -6 to 6
- child_tiles: bfloat16 [64, 128, 2048], P(('front', 'row', 'col')), may hold values from -0.125 to 0.125
- parent_front: int32 [64, 1], P(('front', 'row', 'col')), may hold values from 0 to 3; in each aligned block of 2 rows (0 to 1, 2 to 3, ...) at most 2 rows name the same one
- parent_tile: int32 [64], P(('front', 'row', 'col')), may hold values from 0 to 15
- column_tiles: int32 [64, 16], P(('front', 'row', 'col')), may hold values from 0 to 63
- ranks: int32 [4, 4], P('front', 'row'), may hold values from 128 to 256
Outputs:
- sampled: float32 [4, 2048, 256], P('front', ('row', 'col'))
- bases: float32 [4, 2048, 256], P('front', ('row', 'col'))
The draws below stay inside these ranges and needn't reach their ends.
Inputs may be any that keep to these rules, and one draw needn't show every extreme that they name: `parent_front`: among the 2 tiles of one device, at most 2 name the same parent front.
All inputs are finite; a program needn't handle non-finite values.
Results may differ from the reference program's by a relative error of at most 0.0003.
Values may be sent and summed in bfloat16 or wider, within the bound.
A program may use at most 64 MiB of HBM per device.

```python
import math
import jax
import jax.numpy as jnp
import numpy as np
from jax import lax

F = 8192
S = 256
LEAF = 512
CW = 2048
TILE_DEV = 2
ROWS = 2048
ROW_TILES = 16
PARENTS = 4
CAP = 2
TILES = 64
N_ROW = 4
N_COL = 2


def touch_ends(result, stream_key, low, largest):
    longest = result.shape.index(max(result.shape))
    spots = []
    for shift in (0, 1):
        where = [jax.random.randint(jax.random.fold_in(stream_key, axis), (), 0, length) for axis, length in enumerate(result.shape)]
        where[longest] = (where[longest] + shift) % result.shape[longest]
        spots.append(tuple(where))
    return result.at[spots[0]].set(low).at[spots[1]].set(largest)


def shard_levels(rng, extent, cuts, smallest, largest):
    factor_of, own = 1.0, jax.random.fold_in(rng, 6)
    for axis_at, parts in cuts:
        heights = jnp.exp(jax.random.uniform(jax.random.fold_in(own, axis_at), (parts,), jnp.float32, smallest / len(cuts), largest / len(cuts)))
        factor_of = factor_of * jnp.repeat(heights, extent[axis_at] // parts).reshape([-1 if axis == axis_at else 1 for axis in range(len(extent))])
    return factor_of


def routed_block(stream_key, own, number, rows, amount, top, reach, lean):
    ranking = jax.random.permutation(stream_key, amount)
    packed, ordinary = portions_of(amount, rows * top, reach, lean, True), portions_of(amount, rows * top, reach, lean, False)
    places = jnp.arange(amount)

    def named(sizes, offset_by):
        used = int((sizes > 0).sum())
        fixed = max(1, used // 4)
        shifted = fixed + (places - fixed + offset_by * (used - fixed)) % max(1, amount - fixed)
        return jnp.zeros((amount,), jnp.int32).at[ranking[jnp.where(places < fixed, places, shifted)]].set(jnp.asarray(sizes, jnp.int32))

    sizes = jnp.where(number % 4 == 0, named(packed, number // 4), named(ordinary, number - number // 4 - 1))
    mixed = jax.random.permutation(jax.random.fold_in(own, 3), amount)
    source_of, taker = mixed[0:amount // 2 * 2:2], mixed[1:amount // 2 * 2:2]
    margin = jnp.minimum(sizes[source_of] - 1, reach - sizes[taker]) // 2
    margin = jnp.where((source_of == ranking[0]) | (taker == ranking[0]) | (sizes[taker] == 0), 0, jnp.maximum(margin, 0))
    shifted = jax.random.randint(jax.random.fold_in(own, 4), (amount // 2,), 0, 1 << 20) % (margin + 1)
    sizes = sizes.at[source_of].add(-shifted).at[taker].add(shifted)
    items = jnp.searchsorted(jnp.cumsum(sizes), jnp.arange(rows * top), side="right").astype(jnp.int32)
    grid = items.reshape(top, rows).T
    grid = grid[jax.random.permutation(jax.random.fold_in(own, 1), rows)]
    offset_by = jax.random.randint(jax.random.fold_in(own, 2), (rows, 1), 0, top)
    return jnp.take_along_axis(grid, (jnp.arange(top)[None, :] + offset_by) % top, axis=1)


def portions_of(count, total, most, lean, full):
    loads = [(1 << 20) // math.isqrt(standing ** lean) + 1 for standing in range(1, count + 1)]
    largest = most if full else min(most, max(-(-total // count), total * loads[0] // sum(loads)))
    least = 1 if total - largest >= count - 1 else 0
    holding, surplus = [largest] + [least] * (count - 1), total - largest - least * (count - 1)
    while surplus > 0:
        candidates = [i for i in range(1, count) if holding[i] < largest] or [i for i in range(1, count) if holding[i] < most]
        whole, budget = sum([loads[i] for i in candidates]), surplus
        for i in candidates:
            addition = min(most - holding[i], max(1, budget * loads[i] // whole), surplus)
            holding[i] = holding[i] + addition
            surplus = surplus - addition
    return np.array(holding)


def normal_values(key, extent, scale, most, cuts=(), kind=jnp.bfloat16):
    array = jax.random.normal(key, extent, jnp.float32) * scale
    if len(cuts) > 0:
        array = shard_levels(key, extent, cuts, -0.22, 0.18) * array
    return jnp.clip(array, min=-most, max=most).astype(kind)


def setup_inputs(seed: int = 0) -> dict:
    key_list = jax.random.split(jax.random.key(seed), 8)
    front_slab = normal_values(key_list[0], (PARENTS, ROWS, F), F ** -0.5, 0.0625, ((0, 4), (1, 4), (2, 2)))
    samples = normal_values(key_list[1], (F, S), 1.0, 6.0, ((0, 8),))
    child_tiles = normal_values(key_list[2], (TILES, 128, CW), (CW * TILE_DEV * N_ROW * N_COL // ROW_TILES) ** -0.5, 0.125, ((0, 32),))
    parent_front_keys = jax.random.split(jax.random.fold_in(key_list[3], 1), TILES // TILE_DEV)
    parent_front_turns = jax.random.permutation(jax.random.fold_in(key_list[3], 3), TILES // TILE_DEV)
    parent_front = jax.vmap(lambda own, number: routed_block(jax.random.fold_in(key_list[3], 2), own, number, TILE_DEV, PARENTS, 1, CAP, 2))(parent_front_keys, parent_front_turns).reshape((TILES, 1))
    parent_tile = touch_ends(jax.random.randint(key_list[4], (TILES,), 0, ROW_TILES), jax.random.fold_in(key_list[4], 1), 0, ROW_TILES - 1).astype(jnp.int32)
    column_tiles = touch_ends(jax.random.randint(key_list[5], (TILES, CW // 128), 0, F // 128), jax.random.fold_in(key_list[5], 1), 0, (F // 128) - 1).astype(jnp.int32)
    ranks = touch_ends(jax.random.randint(key_list[6], (PARENTS, N_ROW), S // 2, S + 1), jax.random.fold_in(key_list[6], 1), S // 2, S).astype(jnp.int32)
    return dict(front_slab=front_slab, samples=samples, child_tiles=child_tiles, parent_front=parent_front, parent_tile=parent_tile, column_tiles=column_tiles, ranks=ranks)


def leaf_basis(block, rank):
    width = block.shape[1]
    mask = (jnp.arange(width, dtype=jnp.int32) < rank).astype(jnp.float32)
    masked = block * mask[None, :]
    gram = jnp.dot(masked.T, masked, precision=lax.Precision.HIGHEST)
    gram = gram + jnp.diag(1.0 - mask)
    lower = jnp.linalg.cholesky(gram)
    return lax.linalg.triangular_solve(lower, masked, left_side=False, lower=True, transpose_a=True)

def reference(front_slab, samples, child_tiles, parent_front, parent_tile, column_tiles, ranks):
    parents = front_slab.shape[0]
    rows = front_slab.shape[1]
    full = front_slab.shape[2]
    width = samples.shape[1]
    tile_cols = child_tiles.shape[2]
    blocks = tile_cols // 128
    row_tiles = rows // 128
    omega_tiles = samples.reshape(full // 128, 128, width)
    devices = child_tiles.shape[0] // TILE_DEV
    tiles_blk = child_tiles.reshape(devices, TILE_DEV, 128, blocks, 128)
    dest_blk = parent_front.reshape(devices, TILE_DEV)
    place_blk = parent_tile.reshape(devices, TILE_DEV)
    cols_blk = column_tiles.reshape(devices, TILE_DEV, blocks)

    def step(acc, item):
        pieces, dest, place, cols = item
        chosen = omega_tiles[cols].astype(jnp.float32)
        product = jnp.einsum('trkc,tkcs->trs', pieces.astype(jnp.float32), chosen)
        key = (dest * row_tiles + place).astype(jnp.int32)
        return (acc.at[key].add(product), None)
    start = jnp.zeros((parents * row_tiles, 128, width), jnp.float32)
    extended, _ = lax.scan(step, start, (tiles_blk, dest_blk, place_blk, cols_blk))
    direct = lax.map(lambda slab: jnp.dot(slab.astype(jnp.float32), samples.astype(jnp.float32), preferred_element_type=jnp.float32), front_slab)
    sampled = direct + extended.reshape(parents, rows, width)
    leaves = sampled.reshape(parents * N_ROW, LEAF, width)
    bases = jax.vmap(leaf_basis)(leaves, ranks.reshape(-1))
    return (sampled, bases.reshape(parents, rows, width))
```

```python
import functools

import jax
import jax.numpy as jnp
from jax import lax
from jax.experimental import pallas as pl
from jax.experimental.pallas import tpu as pltpu
from jax.sharding import PartitionSpec as P

F32 = jnp.float32
HI = lax.Precision.HIGHEST
LOGICAL = pl.DeviceIdType.MESH


def dot_nt(a, b):
    return lax.dot_general(a, b, (((1,), (1,)), ((), ())), precision=HI, preferred_element_type=F32)


def inverse_factor(a):
    n = a.shape[0]
    tiles = n // 8
    w = [a[8 * t : 8 * t + 8, :] for t in range(tiles)]
    lane = lax.broadcasted_iota(jnp.int32, (8, n), 1)
    sub = lax.broadcasted_iota(jnp.int32, (8, n), 0)
    rows = []
    for t in range(tiles):
        base = 8 * t
        inside = (lane >= base) & (lane < base + 8)
        cols = [jnp.broadcast_to(w[t][:, base + k : base + k + 1], (8, n)) for k in range(8)]
        v = jnp.where(inside, jnp.where(lane - base == sub, 1.0, 0.0), w[t])
        done, pivots = v, cols[0]
        for k in range(8):
            here = sub == k
            pivot = jnp.broadcast_to(cols[k][k : k + 1, :], (8, n))
            inv = 1.0 / pivot
            done = jnp.where(here, v, done)
            pivots = jnp.where(here, pivot, pivots)
            step = jnp.broadcast_to(v[k : k + 1, :], (8, n)) * inv
            v = jnp.where(here, step, v - cols[k] * step)
            for m in range(k + 1, 8):
                step = jnp.broadcast_to(cols[m][k : k + 1, :], (8, n)) * inv
                cols[m] = jnp.where(here, step, cols[m] - cols[k] * step)
        rows.append(jnp.where(lane < base + 8, done, 0.0) * lax.rsqrt(pivots))
        vk = [jnp.broadcast_to(v[k : k + 1, :], (8, n)) for k in range(8)]
        for u in range(t + 1, tiles):
            x = jnp.where(inside, 0.0, w[u])
            terms = [
                jnp.broadcast_to(w[u][:, base + k : base + k + 1], (8, n)) * vk[k] for k in range(8)
            ]
            low = (terms[0] + terms[1]) + (terms[2] + terms[3])
            high = (terms[4] + terms[5]) + (terms[6] + terms[7])
            w[u] = x - (low + high)
    return jnp.concatenate(rows, axis=0)


def basis_kernel(rank_ref, sampled_ref, gram_ref, out_ref, basis_ref):
    half = gram_ref.shape[1]
    rank = rank_ref[0, 0]
    sampled = sampled_ref[...]
    out_ref[...] = sampled
    rows = sampled.shape[0]
    lane = lax.broadcasted_iota(jnp.int32, (rows, half), 1)
    first = jnp.where(lane < rank, sampled[:, :half], 0.0)
    second = jnp.where(lane + half < rank, sampled[:, half:], 0.0)
    r = lax.broadcasted_iota(jnp.int32, (half, half), 0)
    c = lax.broadcasted_iota(jnp.int32, (half, half), 1)
    a = gram_ref[0] + jnp.where((r == c) & (c >= rank), 1.0, 0.0)
    inv1 = inverse_factor(a)
    low = dot_nt(gram_ref[1], inv1)
    a = gram_ref[2] + jnp.where((r == c) & (c + half >= rank), 1.0, 0.0) - dot_nt(low, low)
    inv2 = inverse_factor(a)
    basis = dot_nt(first, inv1)
    basis_ref[:, :half] = basis
    basis_ref[:, half:] = dot_nt(second - dot_nt(basis, low), inv2)


def leaf_bases(sampled, gram, ranks):
    vmem = pl.BlockSpec(memory_space=pltpu.VMEM)
    return pl.pallas_call(
        basis_kernel,
        out_shape=(jax.ShapeDtypeStruct(sampled.shape, F32),) * 2,
        in_specs=[pl.BlockSpec(memory_space=pltpu.SMEM), vmem, vmem],
        out_specs=(vmem, vmem),
        name="leaf_bases",
    )(ranks, sampled, gram)


def sample_kernel(
    fronts,
    tile_ref,
    front_ref,
    column_ref,
    rank_ref,
    slab_ref,
    samples_ref,
    child_ref,
    sampled_ref,
    gram_ref,
    omega,
    slab,
    child,
    held,
    part,
    blocks,
    got1,
    got2,
    gram_own,
    gram_got,
    copy_sem,
    gs,
    gr,
    zs_right,
    zs_left,
    zs_pair,
    zr,
    zr_pair,
    es,
    er,
):
    f, r, c = lax.axis_index("front"), lax.axis_index("row"), lax.axis_index("col")
    x, core = r // 2, r % 2
    width = samples_ref.shape[2]
    half = width // 2
    chunk = samples_ref.shape[0]
    hc = chunk // 2
    count = child_ref.shape[0]
    slab_rows, slab_cols = slab_ref.shape
    own_rows = slab_rows // 2
    pieces = own_rows // 128
    row_tiles = slab_rows * 4 // 128
    r_x = (1 - x) * 2 + core
    r_p = x * 2 + (1 - core)
    to_x, to_y, to_p = (f, r_x, c), (f, r, 1 - c), (f, r_p, c)
    right, left = (f + 1, r, c), (f - 1, r, c)

    loads = [
        pltpu.make_async_copy(child_ref, child, copy_sem.at[0]),
        pltpu.make_async_copy(slab_ref, slab, copy_sem.at[1]),
        pltpu.make_async_copy(
            samples_ref, omega.at[pl.ds((r * 2 + c) * chunk, chunk)], copy_sem.at[2]
        ),
    ]
    loads[2].start()
    loads[0].start()
    loads[1].start()

    barrier = pltpu.get_barrier_semaphore()
    for target in (to_x, to_y, to_p):
        pl.semaphore_signal(barrier, inc=1, device_id=target, device_id_type=LOGICAL)

    @pl.when(f < fronts - 1)
    def _():
        pl.semaphore_signal(barrier, inc=1, device_id=right, device_id_type=LOGICAL)

    @pl.when(f > 0)
    def _():
        pl.semaphore_signal(barrier, inc=1, device_id=left, device_id_type=LOGICAL)

    pl.semaphore_wait(barrier, 3 + jnp.minimum(f, 1) + jnp.minimum(fronts - 1 - f, 1))

    def rcopy(src, dst, send, recv, target):
        return pltpu.make_async_remote_copy(
            src_ref=src,
            dst_ref=dst,
            send_sem=send,
            recv_sem=recv,
            device_id=target,
            device_id_type=LOGICAL,
        )

    def where_is(row, col, h):
        return pl.ds((row * 2 + col) * chunk + h * hc, hc)

    sent = []

    def send(src, place, n, target):
        cp = rcopy(src, omega.at[place], gs.at[n], gr.at[n], target)
        cp.start()
        sent.append(cp)

    def arrived(place, n):
        rcopy(omega.at[place], omega.at[place], gs.at[n], gr.at[n], to_p).wait_recv()

    own = [samples_ref.at[pl.ds(h * hc, hc)] for h in range(2)]
    for h in (0, 1):
        send(own[h], where_is(r, c, h), h, to_x)
        send(own[1 - h], where_is(r, c, 1 - h), 2 + 1 - h, to_y)
        send(own[h], where_is(r, c, h), 6 + h, to_p)
    place = where_is(r_x, c, 0)
    arrived(place, 0)
    send(omega.at[place], place, 4, to_y)
    send(omega.at[place], place, 8, to_p)
    place = where_is(r, 1 - c, 1)
    arrived(place, 3)
    send(omega.at[place], place, 5, to_x)
    send(omega.at[place], place, 11, to_p)
    place = where_is(r_x, c, 1)
    arrived(place, 1)
    send(omega.at[place], place, 9, to_p)
    place = where_is(r, 1 - c, 0)
    arrived(place, 2)
    send(omega.at[place], place, 10, to_p)
    for h in (0, 1):
        place = where_is(r_x, 1 - c, h)
        arrived(place, 4 + h)
        send(omega.at[place], place, 12 + h, to_p)
    for h in (0, 1):
        arrived(where_is(r_p, c, h), 6 + h)
        arrived(where_is(r_x + r_p - r, c, h), 8 + h)
        arrived(where_is(r_p, 1 - c, h), 10 + h)
        arrived(where_is(r_x + r_p - r, 1 - c, h), 12 + h)
    loads[2].wait()
    loads[0].wait()

    group = 2
    for t in range(count):
        acc = jnp.zeros((128, width), F32)
        for b in range(0, column_ref.shape[1], group):
            chosen = jnp.concatenate(
                [
                    omega[column_ref[t, b + g]]
                    for g in range(group)
                ],
                axis=0,
            )
            acc = acc + jnp.dot(
                child[t, :, 128 * b : 128 * (b + group)], chosen, preferred_element_type=F32
            )
        held[0, f, 128 * t : 128 * (t + 1), :] = acc
        label = (front_ref[t, 0] * row_tiles + tile_ref[t]).astype(F32)
        at = 128 * count + 8 * t
        held[0, f, at : at + 8, :] = jnp.full((8, width), label, F32)

    def along(src, sem, target):
        return rcopy(held.at[0, src], held.at[0, src], sem.at[src], zr.at[src], target)

    def across(src):
        return rcopy(held.at[0, src], held.at[1, src], zs_pair.at[src], zr_pair.at[src], to_p)

    @pl.when(f < fronts - 1)
    def _():
        along(f, zs_right, right).start()

    @pl.when(f > 0)
    def _():
        along(f, zs_left, left).start()

    across(f).start()

    loads[1].wait()

    @pl.loop(0, slab_rows // 128)
    def _(i):
        rows = pl.ds(pl.multiple_of(i * 128, 128), 128)
        part[rows, :] = jnp.dot(
            slab[rows, :],
            omega[pl.ds(c * (slab_cols // 128), slab_cols // 128)].reshape(slab_cols, width),
            preferred_element_type=F32,
        )

    for d in range(1, fronts):

        @pl.when(f >= d)
        def _():
            along(f - d, zs_right, right).wait_recv()

            @pl.when(f < fronts - 1)
            def _():
                along(f - d, zs_right, right).start()

            across(f - d).start()

        @pl.when(f + d < fronts)
        def _():
            along(f + d, zs_left, left).wait_recv()

            @pl.when(f > 0)
            def _():
                along(f + d, zs_left, left).start()

            across(f + d).start()

    for s in range(fronts):
        across(s).wait_recv()

    def fill(h, spot, row, col, piece_of_part):
        lanes = slice(h * half, (h + 1) * half)
        first = f * row_tiles + (row * 2 + col) * pieces
        for i in range(pieces):
            wanted = (first + i).astype(F32)
            masks = []
            for side in range(2):
                for s in range(fronts):
                    for t in range(count):
                        at = 128 * count + 8 * t
                        masks.append((side, s, t, held[side, s, at : at + 8, :half] == wanted))

            @pl.loop(0, 4)
            def _(q):
                accs = [jnp.zeros((8, half), F32)] * 4
                if piece_of_part is not None:
                    accs = [
                        part[
                            pl.ds(
                                pl.multiple_of(
                                    piece_of_part * own_rows + i * 128 + q * 32 + 8 * e, 8
                                ),
                                8,
                            ),
                            lanes,
                        ]
                        for e in range(4)
                    ]
                for side, s, t, mask in masks:
                    for e in range(4):
                        rows = pl.ds(pl.multiple_of(128 * t + q * 32 + 8 * e, 8), 8)
                        accs[e] = accs[e] + jnp.where(mask, held[side, s, rows, lanes], 0.0)
                for e in range(4):
                    rows = pl.ds(pl.multiple_of(i * 128 + q * 32 + 8 * e, 8), 8)
                    blocks[h, spot, rows, :] = accs[e]

    two = pl.ds(2, 2)
    fill(0, 2, r_x, c, None)
    fill(0, 3, r_x, 1 - c, None)
    a1 = rcopy(blocks.at[0, two], got1.at[0], es.at[0], er.at[0], to_x)
    a1.start()
    fill(1, 2, r, 1 - c, 1 - c)
    fill(1, 3, r_x, 1 - c, None)
    b1 = rcopy(blocks.at[1, two], got1.at[1], es.at[1], er.at[1], to_y)
    b1.start()
    fill(0, 1, r, 1 - c, 1 - c)
    fill(1, 1, r_x, c, None)
    fill(0, 0, r, c, c)
    fill(1, 0, r, c, c)
    a1.wait_recv()
    blocks[0, 1] = blocks[0, 1] + got1[0, 1]
    a2 = rcopy(blocks.at[0, 1], got2.at[0], es.at[2], er.at[2], to_y)
    a2.start()
    b1.wait_recv()
    blocks[1, 1] = blocks[1, 1] + got1[1, 1]
    b2 = rcopy(blocks.at[1, 1], got2.at[1], es.at[3], er.at[3], to_x)
    b2.start()
    a2.wait_recv()
    b2.wait_recv()
    lane = lax.broadcasted_iota(jnp.int32, (own_rows, half), 1)
    masked = []
    for h in range(2):
        total = (blocks[h, 0] + got1[h, 0]) + got2[h]
        sampled_ref[:, h * half : (h + 1) * half] = total
        masked.append(jnp.where(lane + h * half < rank_ref[0, 0], total, 0.0))
    for n, (i, j) in enumerate(((0, 0), (1, 0), (1, 1))):
        gram_own[n] = lax.dot_general(
            masked[i],
            masked[j],
            (((0,), (0,)), ((), ())),
            precision=HI,
            preferred_element_type=F32,
        )
    g = rcopy(gram_own, gram_got, es.at[4], er.at[4], to_y)
    g.start()
    for cp in sent:
        cp.wait_send()
    for s in range(fronts):
        across(s).wait_send()

        @pl.when((f < fronts - 1) & (f >= s))
        def _():
            along(s, zs_right, right).wait_send()

        @pl.when((f > 0) & (f <= s))
        def _():
            along(s, zs_left, left).wait_send()

    for cp in (a1, b1, a2, b2):
        cp.wait_send()
    g.wait()
    gram_ref[...] = gram_own[...] + gram_got[...]


def sampled_and_gram(
    fronts, slab, samples, child_tiles, parent_front, parent_tile, column_tiles, ranks
):
    width = samples.shape[1]
    half = width // 2
    count = child_tiles.shape[0]
    rows = slab.shape[0] // 2
    smem = pl.BlockSpec(memory_space=pltpu.SMEM)
    hbm = pl.BlockSpec(memory_space=pl.ANY)
    vmem = pl.BlockSpec(memory_space=pltpu.VMEM)
    dma = lambda n: pltpu.SemaphoreType.DMA((n,))
    return pl.pallas_call(
        functools.partial(sample_kernel, fronts),
        out_shape=(
            jax.ShapeDtypeStruct((rows, width), F32),
            jax.ShapeDtypeStruct((3, half, half), F32),
        ),
        in_specs=[smem] * 4 + [hbm] * 3,
        out_specs=(vmem, vmem),
        scratch_shapes=[
            pltpu.VMEM((samples.shape[0] // 128 * 8, 128, width), samples.dtype),
            pltpu.VMEM(slab.shape, slab.dtype),
            pltpu.VMEM(child_tiles.shape, child_tiles.dtype),
            pltpu.VMEM((2, fronts, 136 * count, width), F32),
            pltpu.VMEM((slab.shape[0], width), F32),
            pltpu.VMEM((2, 4, rows, half), F32),
            pltpu.VMEM((2, 2, rows, half), F32),
            pltpu.VMEM((2, rows, half), F32),
            pltpu.VMEM((3, half, half), F32),
            pltpu.VMEM((3, half, half), F32),
            dma(3),
            dma(14),
            dma(14),
            dma(fronts),
            dma(fronts),
            dma(fronts),
            dma(fronts),
            dma(fronts),
            dma(5),
            dma(5),
        ],
        compiler_params=pltpu.CompilerParams(
            collective_id=0, has_side_effects=True, vmem_limit_bytes=48 * 1024 * 1024
        ),
        name="sampled_and_gram",
    )(
        parent_tile,
        parent_front,
        column_tiles,
        ranks,
        slab,
        samples.reshape(-1, 128, width),
        child_tiles,
    )


def sampled_and_gram_any(
    slab, samples, child_tiles, parent_front, parent_tile, column_tiles, ranks
):
    width = samples.shape[1]
    half = width // 2
    col_width = slab.shape[1]
    omega = lax.all_gather(samples, ("row", "col"), axis=0, tiled=True)
    own = lax.dynamic_slice_in_dim(omega, lax.axis_index("col") * col_width, col_width, 0)
    direct = lax.psum_scatter(
        jnp.dot(slab, own, preferred_element_type=F32), "col", scatter_dimension=0, tiled=True
    )
    count = child_tiles.shape[0]
    blocks = child_tiles.shape[2] // 128
    chosen = omega.reshape(-1, 128, width)[column_tiles]
    pieces = child_tiles.reshape(count, 128, blocks, 128)
    product = jnp.einsum("trkc,tkcs->trs", pieces, chosen, preferred_element_type=F32)
    row_tiles = slab.shape[0] * lax.axis_size("row") // 128
    label = (parent_front[:, 0] * row_tiles + parent_tile).astype(F32)
    product = lax.all_gather(product, "front", axis=0, tiled=True)
    label = lax.all_gather(label, "front", axis=0, tiled=True)
    wanted = (lax.axis_index("front") * row_tiles + jnp.arange(row_tiles)).astype(F32)
    spread = (label[:, None] == wanted[None, :]).astype(F32)
    rows_full = jnp.einsum("qj,qrs->jrs", spread, product, precision=HI)
    rows_full = rows_full.reshape(row_tiles * 128, width)
    extended = lax.psum_scatter(rows_full, ("row", "col"), scatter_dimension=0, tiled=True)
    sampled = direct + extended
    masked = jnp.where(jnp.arange(width)[None, :] < ranks[0, 0], sampled, 0.0)
    gram = lax.psum(jnp.dot(masked.T, masked, precision=HI), "col")
    gram = jnp.stack([gram[:half, :half], gram[half:, :half], gram[half:, half:]])
    return sampled, gram


def on_device(
    sizes, front_slab, samples, child_tiles, parent_front, parent_tile, column_tiles, ranks
):
    args = (samples, child_tiles, parent_front, parent_tile, column_tiles, ranks)
    if sizes["row"] == 4 and sizes["col"] == 2:
        sampled, gram = sampled_and_gram(sizes["front"], front_slab[0], *args)
    else:
        sampled, gram = sampled_and_gram_any(front_slab[0], *args)
    sampled, basis = leaf_bases(sampled, gram, ranks)
    return (sampled[None], basis[None])


def solution(mesh):
    in_specs = (
        P("front", "row", "col"),
        P(("row", "col"), None),
        P(("front", "row", "col"), None, None),
        P(("front", "row", "col"), None),
        P(("front", "row", "col")),
        P(("front", "row", "col"), None),
        P("front", "row"),
    )
    out_specs = (P("front", ("row", "col"), None), P("front", ("row", "col"), None))
    return jax.shard_map(
        functools.partial(on_device, dict(mesh.shape)),
        mesh=mesh,
        in_specs=in_specs,
        out_specs=out_specs,
        check_vma=False,
    )
```

```python
import functools

import jax
import jax.numpy as jnp
from jax import lax
from jax.experimental import pallas as pl
from jax.experimental.pallas import tpu as pltpu
from jax.sharding import PartitionSpec as P

F32 = jnp.float32
HI = lax.Precision.HIGHEST
LOGICAL = pl.DeviceIdType.MESH


def dot_nt(a, b):
    return lax.dot_general(a, b, (((1,), (1,)), ((), ())), precision=HI, preferred_element_type=F32)


def inverse_factor(a):
    n = a.shape[0]
    tiles = n // 8
    w = [a[8 * t : 8 * t + 8, :] for t in range(tiles)]
    lane = lax.broadcasted_iota(jnp.int32, (8, n), 1)
    sub = lax.broadcasted_iota(jnp.int32, (8, n), 0)
    rows = []
    for t in range(tiles):
        base = 8 * t
        inside = (lane >= base) & (lane < base + 8)
        cols = [jnp.broadcast_to(w[t][:, base + k : base + k + 1], (8, n)) for k in range(8)]
        v = jnp.where(inside, jnp.where(lane - base == sub, 1.0, 0.0), w[t])
        done, pivots = v, cols[0]
        for k in range(8):
            here = sub == k
            pivot = jnp.broadcast_to(cols[k][k : k + 1, :], (8, n))
            inv = 1.0 / pivot
            done = jnp.where(here, v, done)
            pivots = jnp.where(here, pivot, pivots)
            step = jnp.broadcast_to(v[k : k + 1, :], (8, n)) * inv
            v = jnp.where(here, step, v - cols[k] * step)
            for m in range(k + 1, 8):
                step = jnp.broadcast_to(cols[m][k : k + 1, :], (8, n)) * inv
                cols[m] = jnp.where(here, step, cols[m] - cols[k] * step)
        rows.append(jnp.where(lane < base + 8, done, 0.0) * lax.rsqrt(pivots))
        vk = [jnp.broadcast_to(v[k : k + 1, :], (8, n)) for k in range(8)]
        for u in range(t + 1, tiles):
            x = jnp.where(inside, 0.0, w[u])
            terms = [
                jnp.broadcast_to(w[u][:, base + k : base + k + 1], (8, n)) * vk[k] for k in range(8)
            ]
            low = (terms[0] + terms[1]) + (terms[2] + terms[3])
            high = (terms[4] + terms[5]) + (terms[6] + terms[7])
            w[u] = x - (low + high)
    return jnp.concatenate(rows, axis=0)


def basis_kernel(sampled_ref, gram_ref, out_ref, basis_ref):
    half = gram_ref.shape[2]
    rank = gram_ref[0, half : half + 1, :]
    sampled = sampled_ref[...]
    out_ref[...] = sampled
    rows = sampled.shape[0]
    lane = lax.broadcasted_iota(jnp.int32, (rows, half), 1).astype(F32)
    first = jnp.where(lane < rank, sampled[:, :half], 0.0)
    second = jnp.where(lane + half < rank, sampled[:, half:], 0.0)
    r = lax.broadcasted_iota(jnp.int32, (half, half), 0)
    c = lax.broadcasted_iota(jnp.int32, (half, half), 1)
    lane = c.astype(F32)
    a = gram_ref[0, :half, :] + jnp.where((r == c) & (lane >= rank), 1.0, 0.0)
    inv1 = inverse_factor(a)
    low = dot_nt(gram_ref[1, :half, :], inv1)
    a = gram_ref[2, :half, :] + jnp.where((r == c) & (lane + half >= rank), 1.0, 0.0)
    a = a - dot_nt(low, low)
    inv2 = inverse_factor(a)
    basis = dot_nt(first, inv1)
    basis_ref[:, :half] = basis
    basis_ref[:, half:] = dot_nt(second - dot_nt(basis, low), inv2)


def leaf_bases(sampled, gram):
    vmem = pl.BlockSpec(memory_space=pltpu.VMEM)
    return pl.pallas_call(
        basis_kernel,
        out_shape=(jax.ShapeDtypeStruct(sampled.shape, F32),) * 2,
        in_specs=[vmem, vmem],
        out_specs=(vmem, vmem),
        name="leaf_bases",
    )(sampled, gram)


def sample_kernel(
    fronts,
    tile_hbm,
    front_hbm,
    column_hbm,
    rank_hbm,
    slab_ref,
    samples_ref,
    child_ref,
    sampled_ref,
    gram_ref,
    tile_ref,
    front_ref,
    column_ref,
    rank_ref,
    omega,
    slab,
    child,
    held,
    part,
    blocks,
    got1,
    got2,
    gram_own,
    gram_got,
    copy_sem,
    gs,
    gr,
    zs_right,
    zs_left,
    zs_pair,
    zr,
    zr_pair,
    es,
    er,
):
    f, r, c = lax.axis_index("front"), lax.axis_index("row"), lax.axis_index("col")
    x, core = r // 2, r % 2
    width = samples_ref.shape[2]
    half = width // 2
    chunk = samples_ref.shape[0]
    piece = chunk // 4
    odd = f % 2
    count = child_ref.shape[0]
    slab_rows, slab_cols = slab_ref.shape
    own_rows = slab_rows // 2
    pieces = own_rows // 128
    row_tiles = slab_rows * 4 // 128
    r_x = (1 - x) * 2 + core
    r_p = x * 2 + (1 - core)
    to_x, to_y, to_p = (f, r_x, c), (f, r, 1 - c), (f, r_p, c)
    right, left = (f + 1, r, c), (f - 1, r, c)

    loads = [
        pltpu.make_async_copy(child_ref, child, copy_sem.at[0]),
        pltpu.make_async_copy(slab_ref, slab, copy_sem.at[1]),
        pltpu.make_async_copy(
            samples_ref, omega.at[pl.ds((r * 2 + c) * chunk, chunk)], copy_sem.at[2]
        ),
    ]
    small = [
        pltpu.make_async_copy(src, dst, copy_sem.at[3 + n])
        for n, (src, dst) in enumerate(
            (
                (tile_hbm, tile_ref),
                (front_hbm, front_ref),
                (column_hbm, column_ref),
                (rank_hbm, rank_ref),
            )
        )
    ]
    loads[2].start()
    for cp in small:
        cp.start()
    loads[0].start()
    loads[1].start()

    barrier = pltpu.get_barrier_semaphore()
    for target in (to_x, to_y, to_p):
        pl.semaphore_signal(barrier, inc=1, device_id=target, device_id_type=LOGICAL)

    @pl.when(f < fronts - 1)
    def _():
        pl.semaphore_signal(barrier, inc=1, device_id=right, device_id_type=LOGICAL)

    @pl.when(f > 0)
    def _():
        pl.semaphore_signal(barrier, inc=1, device_id=left, device_id_type=LOGICAL)

    pl.semaphore_wait(barrier, 3 + jnp.minimum(f, 1) + jnp.minimum(fronts - 1 - f, 1))

    def rcopy(src, dst, send, recv, target):
        return pltpu.make_async_remote_copy(
            src_ref=src,
            dst_ref=dst,
            send_sem=send,
            recv_sem=recv,
            device_id=target,
            device_id_type=LOGICAL,
        )

    to_z = (f + 1 - 2 * odd, r, c)

    def where_is(row, col, i):
        q = i + odd * (3 - 2 * i)
        return pl.ds((row * 2 + col) * chunk + q * piece, piece)

    sent = []

    def send(place, n, target, src=None):
        src = omega.at[place] if src is None else src
        cp = rcopy(src, omega.at[place], gs.at[n], gr.at[n], target)
        cp.start()
        sent.append(cp)

    def arrived(place, n):
        rcopy(omega.at[place], omega.at[place], gs.at[n], gr.at[n], to_p).wait_recv()

    def own(i):
        return samples_ref.at[pl.ds((i + odd * (3 - 2 * i)) * piece, piece)]

    for i, j in ((0, 1), (1, 0), (2, 2)):
        send(where_is(r, c, i), i, to_x, own(i))
        send(where_is(r, c, j), 3 + j, to_y, own(j))
    for i in range(4):
        send(where_is(r, c, i), 12 + i, to_p, own(i))
    x_at = functools.partial(where_is, r_x, c)
    y_at = functools.partial(where_is, r, 1 - c)
    d_at = functools.partial(where_is, r_x, 1 - c)
    arrived(x_at(0), 0)
    send(x_at(0), 6, to_y)
    send(x_at(0), 8, to_z)
    arrived(y_at(1), 4)
    send(y_at(1), 7, to_x)
    send(x_at(0), 16, to_p)
    send(y_at(1), 21, to_p)
    arrived(y_at(0), 3)
    send(y_at(0), 9, to_z)
    send(y_at(0), 20, to_p)
    arrived(x_at(1), 1)
    send(x_at(1), 17, to_p)
    arrived(x_at(3), 8)
    send(x_at(3), 19, to_p)
    arrived(d_at(0), 6)
    send(d_at(0), 10, to_z)
    send(d_at(0), 24, to_p)
    arrived(d_at(1), 7)
    send(d_at(1), 11, to_z)
    send(d_at(1), 25, to_p)
    arrived(y_at(3), 9)
    send(y_at(3), 23, to_p)
    arrived(x_at(2), 2)
    send(x_at(2), 18, to_p)
    arrived(y_at(2), 5)
    send(y_at(2), 22, to_p)
    arrived(d_at(3), 10)
    send(d_at(3), 27, to_p)
    arrived(d_at(2), 11)
    send(d_at(2), 26, to_p)
    r_d = r_x + r_p - r
    for i in range(4):
        arrived(where_is(r_p, c, i), 12 + i)
        arrived(where_is(r_d, c, i), 16 + i)
        arrived(where_is(r_p, 1 - c, i), 20 + i)
        arrived(where_is(r_d, 1 - c, i), 24 + i)
    for cp in small:
        cp.wait()
    loads[2].wait()
    loads[0].wait()

    def tile_row(p, t):
        return 8 + 64 * (p * count + t)

    group = 2
    labels = jnp.zeros((8, width), F32)
    for t in range(count):
        acc = jnp.zeros((128, width), F32)
        for b in range(0, column_ref.shape[1], group):
            chosen = jnp.concatenate(
                [
                    omega[column_ref[t, b + g]]
                    for g in range(group)
                ],
                axis=0,
            )
            acc = acc + jnp.dot(
                child[t, :, 128 * b : 128 * (b + group)], chosen, preferred_element_type=F32
            )
        for p in range(2):
            at = tile_row(p, t)
            held[0, f, at : at + 64, :] = acc[64 * p : 64 * (p + 1)]
        label = (front_ref[t, 0] * row_tiles + tile_ref[t]).astype(F32)
        labels = jnp.where(lax.broadcasted_iota(jnp.int32, (8, width), 0) == t, label, labels)
    held[0, f, 0:8, :] = labels

    spans = [pl.ds(0, tile_row(1, 0)), pl.ds(tile_row(1, 0), 64 * count)]

    def along(src, p, sem, target):
        ref = held.at[0, src, spans[p]]
        return rcopy(ref, ref, sem.at[p, src], zr.at[p, src], target)

    def across(src, p):
        return rcopy(
            held.at[0, src, spans[p]],
            held.at[1, src, spans[p]],
            zs_pair.at[p, src],
            zr_pair.at[p, src],
            to_p,
        )

    for p in range(2):

        @pl.when(f < fronts - 1)
        def _():
            along(f, p, zs_right, right).start()

        @pl.when(f > 0)
        def _():
            along(f, p, zs_left, left).start()

        across(f, p).start()

    loads[1].wait()

    @pl.loop(0, slab_rows // 128)
    def _(i):
        rows = pl.ds(pl.multiple_of(i * 128, 128), 128)
        part[rows, :] = jnp.dot(
            slab[rows, :],
            omega[pl.ds(c * (slab_cols // 128), slab_cols // 128)].reshape(slab_cols, width),
            preferred_element_type=F32,
        )

    def relay(p):
        for d in range(1, fronts):

            @pl.when(f >= d)
            def _():
                along(f - d, p, zs_right, right).wait_recv()

                @pl.when(f < fronts - 1)
                def _():
                    along(f - d, p, zs_right, right).start()

                across(f - d, p).start()

            @pl.when(f + d < fronts)
            def _():
                along(f + d, p, zs_left, left).wait_recv()

                @pl.when(f > 0)
                def _():
                    along(f + d, p, zs_left, left).start()

                across(f + d, p).start()

        for s in range(fronts):
            across(s, p).wait_recv()

    def fill(p, h, spot, row, col, piece_of_part):
        lanes = slice(h * half, (h + 1) * half)
        first = f * row_tiles + (row * 2 + col) * pieces
        for i in range(pieces):
            wanted = (first + i).astype(F32)
            masks = []
            for side in range(2):
                for s in range(fronts):
                    for t in range(count):
                        label = jnp.broadcast_to(held[side, s, t : t + 1, :half], (8, half))
                        masks.append((side, s, t, label == wanted))

            @pl.loop(0, 2)
            def _(q):
                accs = [jnp.zeros((8, half), F32)] * 4
                if piece_of_part is not None:
                    at = piece_of_part * own_rows + i * 128 + p * 64 + q * 32
                    accs = [part[pl.ds(pl.multiple_of(at + 8 * e, 8), 8), lanes] for e in range(4)]
                for side, s, t, mask in masks:
                    for e in range(4):
                        rows = pl.ds(pl.multiple_of(tile_row(p, t) + q * 32 + 8 * e, 8), 8)
                        accs[e] = accs[e] + jnp.where(mask, held[side, s, rows, lanes], 0.0)
                for e in range(4):
                    rows = pl.ds(pl.multiple_of(i * 64 + q * 32 + 8 * e, 8), 8)
                    blocks[p, h, spot, rows, :] = accs[e]

    two = pl.ds(2, 2)
    first_hop = [
        [
            rcopy(blocks.at[p, h, two], got1.at[p, h], es.at[p, h], er.at[p, h], to)
            for h, to in ((0, to_x), (1, to_y))
        ]
        for p in range(2)
    ]
    second_hop = [
        [
            rcopy(blocks.at[p, h, 1], got2.at[p, h], es.at[p, 2 + h], er.at[p, 2 + h], to)
            for h, to in ((0, to_y), (1, to_x))
        ]
        for p in range(2)
    ]

    def spread(p):
        fill(p, 0, 2, r_x, c, None)
        fill(p, 0, 3, r_x, 1 - c, None)
        first_hop[p][0].start()
        fill(p, 1, 2, r, 1 - c, 1 - c)
        fill(p, 1, 3, r_x, 1 - c, None)
        first_hop[p][1].start()
        fill(p, 0, 1, r, 1 - c, 1 - c)
        fill(p, 1, 1, r_x, c, None)
        fill(p, 0, 0, r, c, c)
        fill(p, 1, 0, r, c, c)

    def forward(p):
        for h in range(2):
            first_hop[p][h].wait_recv()
            blocks[p, h, 1] = blocks[p, h, 1] + got1[p, h, 1]
            second_hop[p][h].start()

    def finish(p):
        for h in range(2):
            second_hop[p][h].wait_recv()
            total = (blocks[p, h, 0] + got1[p, h, 0]) + got2[p, h]
            for i in range(pieces):
                at = i * 128 + p * 64
                sampled_ref[at : at + 64, h * half : (h + 1) * half] = total[64 * i : 64 * (i + 1)]

    relay(0)
    spread(0)
    relay(1)
    forward(0)
    spread(1)
    finish(0)
    forward(1)
    finish(1)
    lane = lax.broadcasted_iota(jnp.int32, (own_rows, half), 1)
    masked = []
    for h in range(2):
        total = sampled_ref[:, h * half : (h + 1) * half]
        masked.append(jnp.where(lane + h * half < rank_ref[0, 0], total, 0.0))
    for n, (i, j) in enumerate(((0, 0), (1, 0), (1, 1))):
        gram_own[n] = lax.dot_general(
            masked[i],
            masked[j],
            (((0,), (0,)), ((), ())),
            precision=HI,
            preferred_element_type=F32,
        )
    g = rcopy(gram_own, gram_got, es.at[0, 4], er.at[0, 4], to_y)
    g.start()
    for cp in sent:
        cp.wait_send()
    for p in range(2):
        for s in range(fronts):
            across(s, p).wait_send()

            @pl.when((f < fronts - 1) & (f >= s))
            def _():
                along(s, p, zs_right, right).wait_send()

            @pl.when((f > 0) & (f <= s))
            def _():
                along(s, p, zs_left, left).wait_send()

        for cp in first_hop[p] + second_hop[p]:
            cp.wait_send()
    g.wait()
    rank = jnp.full((3, 8, half), rank_ref[0, 0].astype(F32), F32)
    gram_ref[:, half : half + 8, :] = rank
    gram_ref[:, :half, :] = gram_own[...] + gram_got[...]


def sampled_and_gram(
    fronts, slab, samples, child_tiles, parent_front, parent_tile, column_tiles, ranks
):
    width = samples.shape[1]
    half = width // 2
    count = child_tiles.shape[0]
    rows = slab.shape[0] // 2
    hbm = pl.BlockSpec(memory_space=pl.ANY)
    vmem = pl.BlockSpec(memory_space=pltpu.VMEM)
    dma = lambda *n: pltpu.SemaphoreType.DMA(n)
    return pl.pallas_call(
        functools.partial(sample_kernel, fronts),
        out_shape=(
            jax.ShapeDtypeStruct((rows, width), F32),
            jax.ShapeDtypeStruct((3, half + 8, half), F32),
        ),
        in_specs=[hbm] * 7,
        out_specs=(vmem, vmem),
        scratch_shapes=[
            pltpu.SMEM(parent_tile.shape, jnp.int32),
            pltpu.SMEM(parent_front.shape, jnp.int32),
            pltpu.SMEM(column_tiles.shape, jnp.int32),
            pltpu.SMEM(ranks.shape, jnp.int32),
            pltpu.VMEM((samples.shape[0] // 128 * 8, 128, width), samples.dtype),
            pltpu.VMEM(slab.shape, slab.dtype),
            pltpu.VMEM(child_tiles.shape, child_tiles.dtype),
            pltpu.VMEM((2, fronts, 128 * count + 8, width), F32),
            pltpu.VMEM((slab.shape[0], width), F32),
            pltpu.VMEM((2, 2, 4, rows // 2, half), F32),
            pltpu.VMEM((2, 2, 2, rows // 2, half), F32),
            pltpu.VMEM((2, 2, rows // 2, half), F32),
            pltpu.VMEM((3, half, half), F32),
            pltpu.VMEM((3, half, half), F32),
            dma(7),
            dma(28),
            dma(28),
            dma(2, fronts),
            dma(2, fronts),
            dma(2, fronts),
            dma(2, fronts),
            dma(2, fronts),
            dma(2, 5),
            dma(2, 5),
        ],
        compiler_params=pltpu.CompilerParams(
            collective_id=0, has_side_effects=True, vmem_limit_bytes=67043328
        ),
        name="sampled_and_gram",
    )(
        parent_tile,
        parent_front,
        column_tiles,
        ranks,
        slab,
        samples.reshape(-1, 128, width),
        child_tiles,
    )


def sampled_and_gram_any(
    slab, samples, child_tiles, parent_front, parent_tile, column_tiles, ranks
):
    width = samples.shape[1]
    half = width // 2
    col_width = slab.shape[1]
    omega = lax.all_gather(samples, ("row", "col"), axis=0, tiled=True)
    own = lax.dynamic_slice_in_dim(omega, lax.axis_index("col") * col_width, col_width, 0)
    direct = lax.psum_scatter(
        jnp.dot(slab, own, preferred_element_type=F32), "col", scatter_dimension=0, tiled=True
    )
    count = child_tiles.shape[0]
    blocks = child_tiles.shape[2] // 128
    chosen = omega.reshape(-1, 128, width)[column_tiles]
    pieces = child_tiles.reshape(count, 128, blocks, 128)
    product = jnp.einsum("trkc,tkcs->trs", pieces, chosen, preferred_element_type=F32)
    row_tiles = slab.shape[0] * lax.axis_size("row") // 128
    label = (parent_front[:, 0] * row_tiles + parent_tile).astype(F32)
    product = lax.all_gather(product, "front", axis=0, tiled=True)
    label = lax.all_gather(label, "front", axis=0, tiled=True)
    wanted = (lax.axis_index("front") * row_tiles + jnp.arange(row_tiles)).astype(F32)
    spread = (label[:, None] == wanted[None, :]).astype(F32)
    rows_full = jnp.einsum("qj,qrs->jrs", spread, product, precision=HI)
    rows_full = rows_full.reshape(row_tiles * 128, width)
    extended = lax.psum_scatter(rows_full, ("row", "col"), scatter_dimension=0, tiled=True)
    sampled = direct + extended
    masked = jnp.where(jnp.arange(width)[None, :] < ranks[0, 0], sampled, 0.0)
    gram = lax.psum(jnp.dot(masked.T, masked, precision=HI), "col")
    gram = jnp.stack([gram[:half, :half], gram[half:, :half], gram[half:, half:]])
    rank = jnp.broadcast_to(ranks.astype(F32)[:, :, None], (3, 8, half))
    return sampled, jnp.concatenate([gram, rank], axis=1)


def on_device(
    sizes, front_slab, samples, child_tiles, parent_front, parent_tile, column_tiles, ranks
):
    args = (samples, child_tiles, parent_front, parent_tile, column_tiles, ranks)
    if sizes["row"] == 4 and sizes["col"] == 2 and sizes["front"] % 2 == 0:
        sampled, gram = sampled_and_gram(sizes["front"], front_slab[0], *args)
    else:
        sampled, gram = sampled_and_gram_any(front_slab[0], *args)
    sampled, basis = leaf_bases(sampled, gram)
    return (sampled[None], basis[None])


def solution(mesh):
    in_specs = (
        P("front", "row", "col"),
        P(("row", "col"), None),
        P(("front", "row", "col"), None, None),
        P(("front", "row", "col"), None),
        P(("front", "row", "col")),
        P(("front", "row", "col"), None),
        P("front", "row"),
    )
    out_specs = (P("front", ("row", "col"), None), P("front", ("row", "col"), None))
    return jax.shard_map(
        functools.partial(on_device, dict(mesh.shape)),
        mesh=mesh,
        in_specs=in_specs,
        out_specs=out_specs,
        check_vma=False,
    )
```
